32 devices in a mesh: dom: 8 (over z, y), group: 4 (over x, core).
Axes of the slice: x: 2, y: 2, z: 4, core: 2. Of those that a mesh axis runs over, the one named last changes fastest.
Arguments:
- features: bfloat16 [4096, 1024], P(('dom', 'group')), may hold values from -6 to 6
- out_grad: bfloat16 [4096, 1024], P(('dom', 'group')), may hold values from -0.1796875 to 0.1796875
- gcn_weight: bfloat16 [1024, 1024], replicated, may hold values from -0.1875 to 0.1875
- tile_index: int32 [32, 4], P(('dom', 'group')), may hold values from 0 to 2
- tile_edges: int32 [32, 4, 128, 128], P(('dom', 'group')), may hold values 0 or 1
- halo_rows: int32 [8, 4, 8, 32], P('dom', 'group'), may hold values from 0 to 127
- routes: int32 [4096, 2], P(('dom', 'group')), may hold values from 0 to 15, all different within a row; in each aligned block of 128 rows (0 to 127, 128 to 255, ...) at most 20 rows name the same one
- route_weight: float32 [4096, 2], P(('dom', 'group')), may hold values from 0.25 to 1
- up_weight: bfloat16 [16, 1024, 4096], P('dom', None, 'group'), may hold values from -0.1875 to 0.1875
- down_weight: bfloat16 [16, 4096, 1024], P('dom', 'group'), may hold values from -0.09375 to 0.09375
Outputs:
- node_out: bfloat16 [4096, 1024], P(('dom', 'group'))
- up_grad: bfloat16 [16, 1024, 4096], P('dom', None, 'group')
- down_grad: bfloat16 [16, 4096, 1024], P('dom', 'group')
The draws below stay inside these ranges and needn't reach their ends.
Inputs may be any that keep to these rules, and one draw needn't show every extreme that they name: `routes`: in the rows of one partition no expert is named more than 20 times, and in every draw some partition names some expert exactly 20 times.
All inputs are finite; a program needn't handle non-finite values. No bound on the sum of `tile_edges` on one device may be relied on, other than what follows from the above.
Results may differ from the reference program's by a relative error of at most 0.0071.
Values may be sent and summed in bfloat16 or wider, within the bound.
A program may use at most 128 MiB of HBM per device.

```python
import math
import jax
import jax.numpy as jnp
import numpy as np
from jax import lax

D = 1024
FF = 4096
TOP = 2
TILE = 128
SLOTS = 4
NODES_DEV = 128
FF_DEV = 1024
EXPERTS = 16
NODES = 4096
LTILES = 1
STILES = 3
HROWS = 32
CAP = 20
N_DOM = 8
N_GROUP = 4


def set_ends(drawn, stream_key, smallest, high):
    spot = [jax.random.randint(jax.random.fold_in(stream_key, axis), (), 0, length) for axis, length in enumerate(drawn.shape)]
    longest = drawn.shape.index(max(drawn.shape))
    neighbour = spot[:longest] + [(spot[longest] + 1) % drawn.shape[longest]] + spot[longest + 1:]
    return drawn.at[tuple(spot)].set(smallest).at[tuple(neighbour)].set(high)


def level_of(stream_key, extent, split, least, high):
    def one(position, blocks):
        draws = jax.random.uniform(jax.random.fold_in(jax.random.fold_in(stream_key, 6), position), (blocks,), jnp.float32, least / len(split), high / len(split))
        return jnp.repeat(jnp.exp(draws), extent[position] // blocks).reshape((-1,) + (1,) * (len(extent) - position - 1))

    level = one(*split[0])
    for cut in split[1:]:
        level = level * one(*cut)
    return level


def deal_out(stream_key, own, number, rows, count, top, bound, slope):
    ranking = jax.random.permutation(stream_key, count)
    crowded, common = portions_of(count, rows * top, bound, slope, True), portions_of(count, rows * top, bound, slope, False)
    places = jnp.arange(count)

    def named(lengths, offset_by):
        used = int((lengths > 0).sum())
        fixed = max(1, used // 4)
        passed = fixed + (places - fixed + offset_by * (used - fixed)) % max(1, count - fixed)
        return jnp.zeros((count,), jnp.int32).at[ranking[jnp.where(places < fixed, places, passed)]].set(jnp.asarray(lengths, jnp.int32))

    lengths = jnp.where(number % 4 == 0, named(crowded, number // 4), named(common, number - number // 4 - 1))
    mixed = jax.random.permutation(jax.random.fold_in(own, 3), count)
    donor, taker = mixed[0:count // 2 * 2:2], mixed[1:count // 2 * 2:2]
    room = jnp.minimum(lengths[donor] - 1, bound - lengths[taker]) // 2
    room = jnp.where((donor == ranking[0]) | (taker == ranking[0]) | (lengths[taker] == 0), 0, jnp.maximum(room, 0))
    passed = jax.random.randint(jax.random.fold_in(own, 4), (count // 2,), 0, 1 << 20) % (room + 1)
    lengths = lengths.at[donor].add(-passed).at[taker].add(passed)
    members = jnp.searchsorted(jnp.cumsum(lengths), jnp.arange(rows * top), side="right").astype(jnp.int32)
    listing = members.reshape(top, rows).T
    listing = listing[jax.random.permutation(jax.random.fold_in(own, 1), rows)]
    offset_by = jax.random.randint(jax.random.fold_in(own, 2), (rows, 1), 0, top)
    return jnp.take_along_axis(listing, (jnp.arange(top)[None, :] + offset_by) % top, axis=1)


def portions_of(count, total, bound, slope, full):
    portions = [(1 << 20) // math.isqrt(rank ** slope) + 1 for rank in range(1, count + 1)]
    largest = bound if full else min(bound, max(-(-total // count), total * portions[0] // sum(portions)))
    least = 1 if total - largest >= count - 1 else 0
    counts, rest = [largest] + [least] * (count - 1), total - largest - least * (count - 1)
    while rest > 0:
        candidates = [i for i in range(1, count) if counts[i] < largest] or [i for i in range(1, count) if counts[i] < bound]
        mass, budget = sum([portions[i] for i in candidates]), rest
        for i in candidates:
            more = min(bound - counts[i], max(1, budget * portions[i] // mass), rest)
            counts[i] = counts[i] + more
            rest = rest - more
    return np.array(counts)


def gaussian(stream_key, extent, scale, most, shards=(), kind=jnp.bfloat16):
    array = scale * jax.random.normal(stream_key, extent, jnp.float32)
    if shards:
        array = array * level_of(stream_key, extent, shards, -0.22, 0.18)
    return jnp.clip(array, -most, most).astype(kind)


def setup_inputs(seed: int = 0) -> dict:
    arg_keys = jax.random.split(jax.random.key(seed), 11)
    features = gaussian(arg_keys[0], (NODES, D), 1.0, 6.0, ((0, 32),))
    out_grad = gaussian(arg_keys[1], (NODES, D), 0.03, 0.1796875, ((0, 32),))
    gcn_weight = gaussian(arg_keys[2], (D, D), D ** -0.5, 0.1875)
    tile_index = set_ends(jax.random.randint(arg_keys[3], (NODES // TILE, SLOTS), 0, STILES), jax.random.fold_in(arg_keys[3], 1), 0, STILES - 1).astype(jnp.int32)
    tile_edges = set_ends((jax.random.randint(arg_keys[4], (NODES // TILE, SLOTS, TILE, TILE), 0, 16) < 1).astype(jnp.int32), jax.random.fold_in(arg_keys[4], 1), 0, 1)
    halo_rows = set_ends(jax.random.randint(arg_keys[5], (N_DOM, N_GROUP, N_DOM, HROWS), 0, NODES_DEV), jax.random.fold_in(arg_keys[5], 1), 0, NODES_DEV - 1).astype(jnp.int32)
    routes_keys = jax.random.split(jax.random.fold_in(arg_keys[6], 1), NODES // NODES_DEV)
    routes_turns = jax.random.permutation(jax.random.fold_in(arg_keys[6], 3), NODES // NODES_DEV)
    routes = jax.vmap(lambda own, number: deal_out(jax.random.fold_in(arg_keys[6], 2), own, number, NODES_DEV, EXPERTS, TOP, CAP, 2))(routes_keys, routes_turns).reshape((NODES, TOP))
    route_weight = jnp.clip(0.25 + 0.75 * jax.random.uniform(arg_keys[7], (NODES, TOP), jnp.float32) ** level_of(arg_keys[7], (NODES, TOP), ((0, 32),), -0.2, 0.2), 0.25, 1.0)
    up_weight = gaussian(arg_keys[8], (EXPERTS, D, FF), D ** -0.5, 0.1875, ((0, 8), (2, 4)))
    down_weight = gaussian(arg_keys[9], (EXPERTS, FF, D), FF ** -0.5, 0.09375, ((0, 8), (1, 4)))
    return dict(features=features, out_grad=out_grad, gcn_weight=gcn_weight, tile_index=tile_index, tile_edges=tile_edges, halo_rows=halo_rows, routes=routes, route_weight=route_weight, up_weight=up_weight, down_weight=down_weight)


def silu_slope(values):
    logistic = jax.nn.sigmoid(values)
    return logistic * (1.0 + values * (1.0 - logistic))

def slot_table(route_rows):
    flat_ids = route_rows.reshape(-1)
    onehot = (flat_ids[:, None] == jnp.arange(EXPERTS, dtype=jnp.int32)[None, :]).astype(jnp.int32)
    before = jnp.cumsum(onehot, axis=0) - onehot
    within = lax.optimization_barrier(jnp.sum(before * onehot, axis=1))
    target = flat_ids * CAP + within
    filler = jnp.zeros((EXPERTS * CAP,), jnp.int32).at[target].set(jnp.arange(flat_ids.shape[0], dtype=jnp.int32) + 1)
    return (target, filler)

def pick_rows(matrix, positions):
    return matrix[positions]

def aggregate(packed):
    source_tiles, index_row, edge_row, own_rows = packed
    chosen = source_tiles[index_row]
    summed = own_rows.reshape(LTILES, TILE, D).astype(jnp.float32) + jnp.einsum('tsij,tsjd->tid', edge_row.astype(jnp.float32), chosen.astype(jnp.float32))
    degree = 1.0 + lax.optimization_barrier(jnp.sum(edge_row, axis=(1, 3))).astype(jnp.float32)
    return (summed / jnp.sqrt(degree)[:, :, None]).reshape(NODES_DEV, D).astype(jnp.bfloat16)

def expert(packed):
    token_rows, cot_rows, up_matrix, down_matrix = packed
    count_rows = token_rows.shape[0]
    up_proj = jnp.dot(token_rows, up_matrix, preferred_element_type=jnp.float32)
    active = jax.nn.silu(up_proj).astype(jnp.bfloat16)
    blocks = jnp.einsum('rgf,gfd->rgd', active.reshape(count_rows, N_GROUP, FF_DEV).astype(jnp.float32), down_matrix.reshape(N_GROUP, FF_DEV, D).astype(jnp.float32))
    rounded = lax.optimization_barrier(blocks.astype(jnp.bfloat16)).astype(jnp.float32)
    expert_out = lax.optimization_barrier(jnp.sum(rounded, axis=1)).astype(jnp.bfloat16)
    grad_act = jnp.dot(cot_rows, down_matrix.T, preferred_element_type=jnp.float32)
    grad_pre = (grad_act * silu_slope(up_proj)).astype(jnp.bfloat16)
    down_part = jnp.dot(active.T, cot_rows, preferred_element_type=jnp.float32).astype(jnp.bfloat16)
    up_part = jnp.dot(token_rows.T, grad_pre, preferred_element_type=jnp.float32).astype(jnp.bfloat16)
    return (expert_out, up_part, down_part)

def reference(features, out_grad, gcn_weight, tile_index, tile_edges, halo_rows, routes, route_weight, up_weight, down_weight):
    devices = N_DOM * N_GROUP
    node_grid = features.reshape(N_DOM, N_GROUP, NODES_DEV, D)
    dom_ids = jnp.arange(N_DOM, dtype=jnp.int32)[:, None, None, None]
    group_ids = jnp.arange(N_GROUP, dtype=jnp.int32)[None, :, None, None]
    picked = node_grid[dom_ids, group_ids, halo_rows]
    border = jnp.transpose(picked, (2, 1, 0, 3, 4)).reshape(devices, N_DOM * HROWS, D)
    own_nodes = features.reshape(devices, NODES_DEV, D)
    sources = jnp.concatenate([own_nodes, border], axis=1).reshape(devices, STILES, TILE, D)
    aggregated = lax.map(aggregate, (sources, tile_index.reshape(devices, LTILES, SLOTS), tile_edges.reshape(devices, LTILES, SLOTS, TILE, TILE), own_nodes)).reshape(NODES, D)
    preact = jnp.dot(aggregated, gcn_weight, preferred_element_type=jnp.float32)
    hidden = (features.astype(jnp.float32) + jax.nn.silu(preact)).astype(jnp.bfloat16)
    targets, fillers = jax.vmap(slot_table)(routes.reshape(devices, NODES_DEV * TOP))
    cotangent = (route_weight[:, :, None] * out_grad[:, None, :].astype(jnp.float32)).astype(jnp.bfloat16).reshape(devices, NODES_DEV * TOP, D)
    hidden_dev = hidden.reshape(devices, NODES_DEV, D)
    present = (fillers > 0)[:, :, None]
    source_pair = jnp.maximum(fillers - 1, 0)
    nothing = jnp.zeros((), jnp.bfloat16)
    slot_hidden = jnp.where(present, jax.vmap(pick_rows)(hidden_dev, source_pair // TOP), nothing)
    slot_cot = jnp.where(present, jax.vmap(pick_rows)(cotangent, source_pair), nothing)
    expert_hidden = jnp.transpose(slot_hidden.reshape(devices, EXPERTS, CAP, D), (1, 0, 2, 3)).reshape(EXPERTS, devices * CAP, D)
    expert_cot = jnp.transpose(slot_cot.reshape(devices, EXPERTS, CAP, D), (1, 0, 2, 3)).reshape(EXPERTS, devices * CAP, D)
    expert_outs, up_grad, down_grad = lax.map(expert, (expert_hidden, expert_cot, up_weight, down_weight))
    returned = jnp.transpose(expert_outs.reshape(EXPERTS, devices, CAP, D), (1, 0, 2, 3)).reshape(devices, EXPERTS * CAP, D)
    gathered = jax.vmap(pick_rows)(returned, targets).reshape(NODES, TOP, D)
    node_out = (hidden.astype(jnp.float32) + lax.optimization_barrier(jnp.sum(route_weight[:, :, None] * gathered.astype(jnp.float32), axis=1))).astype(jnp.bfloat16)
    return (node_out, up_grad, down_grad)
```

```python
import jax
import jax.numpy as jnp
from jax import lax
from jax.sharding import PartitionSpec as P


def silu_slope(values):
    logistic = jax.nn.sigmoid(values)
    return logistic * (1.0 + values * (1.0 - logistic))


def slot_table(route_rows, expert_count, capacity):
    flat_ids = route_rows.reshape(-1)
    onehot = (flat_ids[:, None] == jnp.arange(expert_count, dtype=jnp.int32)[None, :]).astype(
        jnp.int32
    )
    before = jnp.cumsum(onehot, axis=0) - onehot
    within = jnp.sum(before * onehot, axis=1)
    target = flat_ids * capacity + within
    filler = (
        jnp.zeros((expert_count * capacity,), jnp.int32)
        .at[target]
        .set(jnp.arange(flat_ids.shape[0], dtype=jnp.int32) + 1)
    )
    return (target, filler)


def local(
    features,
    out_grad,
    gcn_weight,
    tile_index,
    tile_edges,
    halo_rows,
    routes,
    route_weight,
    up_weight,
    down_weight,
):
    dom_count = lax.axis_size("dom")
    group_count = lax.axis_size("group")
    node_count, width = features.shape
    tile_rows = tile_edges.shape[-1]
    local_tiles = tile_index.shape[0]
    border_rows = halo_rows.shape[-1]
    expert_local = up_weight.shape[0]
    expert_count = expert_local * dom_count
    top_count = routes.shape[1]
    capacity = max(2, 5 * node_count * top_count // (4 * expert_count))
    send_lists = halo_rows.reshape(-1)
    outgoing = features[send_lists].reshape(dom_count, border_rows, width)
    incoming = lax.all_to_all(outgoing, "dom", split_axis=0, concat_axis=0, tiled=True)
    sources = jnp.concatenate(
        [features, incoming.reshape(dom_count * border_rows, width)], axis=0
    ).reshape(-1, tile_rows, width)
    chosen = sources[tile_index]
    edge_values = tile_edges.astype(jnp.bfloat16)
    summed = features.reshape(local_tiles, tile_rows, width).astype(jnp.float32) + jnp.einsum(
        "tsij,tsjd->tid", edge_values, chosen, preferred_element_type=jnp.float32
    )
    degree = 1.0 + jnp.sum(tile_edges, axis=(1, 3)).astype(jnp.float32)
    aggregated = (
        (summed / jnp.sqrt(degree)[:, :, None]).reshape(node_count, width).astype(jnp.bfloat16)
    )
    preact = jnp.dot(aggregated, gcn_weight, preferred_element_type=jnp.float32)
    hidden = (features.astype(jnp.float32) + jax.nn.silu(preact)).astype(jnp.bfloat16)
    targets, fillers = slot_table(routes, expert_count, capacity)
    cotangent = (
        (route_weight[:, :, None] * out_grad[:, None, :].astype(jnp.float32))
        .astype(jnp.bfloat16)
        .reshape(-1, width)
    )
    present = (fillers > 0)[:, None]
    source_pair = jnp.maximum(fillers - 1, 0)
    nothing = jnp.zeros((), jnp.bfloat16)
    slot_shape = (dom_count, expert_local * capacity, width)
    send_hidden = jnp.where(present, hidden[source_pair // top_count], nothing).reshape(slot_shape)
    send_cot = jnp.where(present, cotangent[source_pair], nothing).reshape(slot_shape)
    mine_cot = lax.all_to_all(send_cot, "dom", split_axis=0, concat_axis=0, tiled=True)
    token_cot = lax.all_gather(mine_cot[None], "group", axis=0, tiled=True)
    mine_hidden = lax.all_to_all(send_hidden, "dom", split_axis=0, concat_axis=0, tiled=True)
    token_hidden = lax.all_gather(mine_hidden[None], "group", axis=0, tiled=True)
    sender_count = group_count * dom_count
    token_hidden = token_hidden.reshape(sender_count, expert_local, capacity, width)
    token_cot = token_cot.reshape(sender_count, expert_local, capacity, width)
    up_proj = jnp.einsum(
        "secd,edf->secf", token_hidden, up_weight, preferred_element_type=jnp.float32
    )
    active = jax.nn.silu(up_proj).astype(jnp.bfloat16)
    merged = lax.psum_scatter(
        jnp.einsum(
            "secf,efd->secd", active, down_weight, preferred_element_type=jnp.float32
        ).astype(jnp.bfloat16),
        "group",
        scatter_dimension=0,
        tiled=True,
    )
    expert_out = merged.reshape(dom_count, expert_local * capacity, width)
    returned = lax.all_to_all(expert_out, "dom", split_axis=0, concat_axis=0, tiled=True).reshape(
        expert_count * capacity, width
    )
    gathered = returned[targets].reshape(node_count, top_count, width)
    node_out = (
        hidden.astype(jnp.float32)
        + jnp.sum(route_weight[:, :, None] * gathered.astype(jnp.float32), axis=1)
    ).astype(jnp.bfloat16)
    grad_act = jnp.einsum(
        "secd,efd->secf", token_cot, down_weight, preferred_element_type=jnp.float32
    )
    grad_pre = (grad_act * silu_slope(up_proj)).astype(jnp.bfloat16)
    down_grad = jnp.einsum(
        "secf,secd->efd", active, token_cot, preferred_element_type=jnp.float32
    ).astype(jnp.bfloat16)
    up_grad = jnp.einsum(
        "secd,secf->edf", token_hidden, grad_pre, preferred_element_type=jnp.float32
    ).astype(jnp.bfloat16)
    return (node_out, up_grad, down_grad)


def solution(mesh):
    in_specs = (
        P(("dom", "group"), None),
        P(("dom", "group"), None),
        P(),
        P(("dom", "group"), None),
        P(("dom", "group"), None, None, None),
        P("dom", "group", None, None),
        P(("dom", "group"), None),
        P(("dom", "group"), None),
        P("dom", None, "group"),
        P("dom", "group", None),
    )
    out_specs = (P(("dom", "group"), None), P("dom", None, "group"), P("dom", "group", None))
    return jax.shard_map(local, mesh=mesh, in_specs=in_specs, out_specs=out_specs, check_vma=False)
```
